256 devices in a mesh: section: 16 (over z_hi, x, core), blk: 16 (over y, z_lo).
Axes of the slice: x: 4, y: 4, z: 8 (z_hi: 2, z_lo: 4; z = z_hi * 4 + z_lo), core: 2. Of those that a mesh axis runs over, the one named last changes fastest.
Arguments:
- queries: bfloat16 [16, 2048, 4096], P('section', 'blk'), may hold values from -6 to 6
- key_heads: bfloat16 [16, 2048, 512], P('section', 'blk'), may hold values from -6 to 6
- value_per_head: bfloat16 [16, 2048, 512], P('section', 'blk'), may hold values from -6 to 6
- out_grads: bfloat16 [16, 2048, 4096], P('section', 'blk'), may hold values from -6 to 6
- segment_ids: int32 [16, 2048], P('section', 'blk'), may hold values from 0 to 127, never falling along the last dimension, each value on 1 to 64 neighbouring positions
- block_lists: int32 [16, 16, 4], P('section', 'blk'), may hold values from 0 to 15, as said below
- list_counts: int32 [16, 16], P('section', 'blk'), may hold values from 1 to 4, as said below
Outputs:
- grad_queries: bfloat16 [16, 2048, 4096], P('section', 'blk')
- grad_keys: bfloat16 [16, 2048, 512], P('section', 'blk')
- grad_values: bfloat16 [16, 2048, 512], P('section', 'blk')
The draws below stay inside these ranges and needn't reach their ends.
Inputs may be any that keep to these rules, and one draw needn't show every extreme that they name: `block_lists`: entry 0 of row b is b itself; for b >= 1 entry 1 is block 0; entries 2 to list_counts - 1 are distinct blocks between 1 and b - 1; entries from list_counts on repeat b. `list_counts`: at least 2 for every query block after the first; the last query block of every micro-batch uses all 4 slots.
All inputs are finite; a program needn't handle non-finite values.
Results may differ from the reference program's by a relative error of at most 0.0051.
Values may be sent and summed in bfloat16 or wider, within the bound.
A program may use at most 64 MiB of HBM per device.

```python
import math
import jax
import jax.numpy as jnp
import numpy as np
from jax import lax

QUERY_HEADS = 32
KEY_VALUE_HEADS = 4
HEAD_SIZE = 128
MASK_BLOCK_SIZE = 128
LIST = 4
QUERY_BLOCKS = 16
MICRO_POSITIONS = 2048
MICRO_BATCHES = 16


def draw_queries(key, part):
    random_root_key = jax.random.fold_in(key, 1)
    value_tensor = jax.random.truncated_normal(random_root_key, -6.0, 6.0, (MICRO_BATCHES, MICRO_POSITIONS, QUERY_HEADS * HEAD_SIZE), jnp.float32)
    return value_tensor.astype(jnp.bfloat16)


def draw_key_heads(key, part):
    random_root_key = jax.random.fold_in(key, 2)
    value_tensor = jax.random.truncated_normal(random_root_key, -6.0, 6.0, (MICRO_BATCHES, MICRO_POSITIONS, KEY_VALUE_HEADS * HEAD_SIZE), jnp.float32)
    return value_tensor.astype(jnp.bfloat16)


def list_tables(key):
    table_key = jax.random.fold_in(key, 7)
    score_key, count_key = jax.random.split(table_key)
    column = jnp.arange(QUERY_BLOCKS, dtype=jnp.int32)
    raw_scores = jax.random.randint(score_key, (MICRO_BATCHES, QUERY_BLOCKS, QUERY_BLOCKS), 0, 1 << 20, jnp.int32) * QUERY_BLOCKS + column[None, None, :]
    row_block = column[None, :, None]
    valid = (column[None, None, :] >= 1) & (column[None, None, :] < row_block)
    masked = jnp.where(valid, raw_scores, (1 << 30) + column[None, None, :])
    order = jnp.argsort(masked, axis=-1, stable=True)[..., :LIST - 2].astype(jnp.int32)
    wanted = jax.random.randint(count_key, (MICRO_BATCHES, QUERY_BLOCKS), 2, LIST + 1, jnp.int32)
    query_block = column[None, :]
    upper = jnp.minimum(LIST, query_block + 1)
    lower = jnp.minimum(2, query_block + 1)
    counts = jnp.clip(wanted, lower, upper)
    counts = jnp.where(query_block == QUERY_BLOCKS - 1, upper, counts)
    own = jnp.broadcast_to(query_block[..., None], (MICRO_BATCHES, QUERY_BLOCKS, 1))
    entries = jnp.concatenate([own, jnp.zeros((MICRO_BATCHES, QUERY_BLOCKS, 1), jnp.int32), order], axis=-1)[..., :LIST]
    slots = jnp.arange(LIST, dtype=jnp.int32)
    entries = jnp.where(slots[None, None, :] < counts[..., None], entries, own)
    return (entries.astype(jnp.int32), counts.astype(jnp.int32))


def draw_block_lists(key, part):
    return list_tables(key)[0]


def draw_list_counts(key, part):
    return list_tables(key)[1]


def shard_levels(stream_key, extent, cuts, low, high):
    level = 1.0
    for position, parts in cuts:
        draws = jax.random.uniform(jax.random.fold_in(jax.random.fold_in(stream_key, 6), position), (parts,), jnp.float32, low / len(cuts), high / len(cuts))
        level = level * jnp.repeat(jnp.exp(draws), extent[position] // parts).reshape((-1,) + (1,) * (len(extent) - 1 - position))
    return level


def length_profile(number_of, total, most, slope):
    portions = [(1 << 20) // math.isqrt(standing ** slope) + 1 for standing in range(2, number_of + 1)]
    spare, given = total - most - (number_of - 1), [1] * (number_of - 1)
    while spare > 0:
        candidates = [i for i in range(number_of - 1) if given[i] < most]
        mass, budget = sum([portions[i] for i in candidates]), spare
        for i in candidates:
            addition = min(most - given[i], max(1, budget * portions[i] // mass), spare)
            given[i] = given[i] + addition
            spare = spare - addition
    return np.array([most] + given)


def uneven(stream_key, number_of, total, most, slope):
    if number_of == 2:
        one = jax.random.randint(stream_key, (), max(1, total - most), min(most, total - 1) + 1)
        return jnp.stack([one, total - one])
    lengths = jnp.asarray(length_profile(number_of, total, most, slope), jnp.int32)
    pairs = (number_of - 1) // 2
    giver, taker = lengths[1:1 + 2 * pairs:2], lengths[2:2 + 2 * pairs:2]
    room = jnp.minimum(giver - 1, most - taker)
    passed = jax.random.randint(jax.random.fold_in(stream_key, 1), (pairs,), 0, 1 << 20) % (room + 1)
    lengths = lengths.at[1:1 + 2 * pairs:2].set(giver - passed).at[2:2 + 2 * pairs:2].set(taker + passed)
    return lengths[jax.random.permutation(jax.random.fold_in(stream_key, 2), number_of)]


def gaussian(own_key, shape, scale, reach, shards=(), kind=jnp.bfloat16):
    values = jax.random.normal(own_key, shape, jnp.float32) * scale
    if len(shards) > 0:
        values = shard_levels(own_key, shape, shards, -0.22, 0.18) * values
    return jnp.clip(values, min=-reach, max=reach).astype(kind)


def setup_inputs(seed: int = 0) -> dict:
    keys = jax.random.split(jax.random.key(seed), 8)
    queries = draw_queries(jax.random.fold_in(keys[7], 71), 0)
    key_heads = draw_key_heads(jax.random.fold_in(keys[7], 71), 0)
    value_per_head = gaussian(keys[2], (MICRO_BATCHES, MICRO_POSITIONS, KEY_VALUE_HEADS * HEAD_SIZE), 1.0, 6.0, ((0, 16), (1, 16)))
    out_grads = gaussian(keys[3], (MICRO_BATCHES, MICRO_POSITIONS, QUERY_HEADS * HEAD_SIZE), 1.0, 6.0, ((0, 16), (1, 16)))
    segment_ids = jax.vmap(lambda own: jnp.searchsorted(jnp.cumsum(uneven(own, MICRO_POSITIONS // 16, MICRO_POSITIONS, 64, 2)), jnp.arange(MICRO_POSITIONS), side="right"))(jax.random.split(keys[4], MICRO_BATCHES)).reshape((MICRO_BATCHES, MICRO_POSITIONS)).astype(jnp.int32)
    block_lists = draw_block_lists(jax.random.fold_in(keys[7], 71), 0)
    list_counts = draw_list_counts(jax.random.fold_in(keys[7], 71), 0)
    return {"queries": queries, "key_heads": key_heads, "value_per_head": value_per_head, "out_grads": out_grads, "segment_ids": segment_ids, "block_lists": block_lists, "list_counts": list_counts}


NEG_FILL = -1e+30

def allowed_mask(block_ids, listed_count, query_block, query_segs):
    slot_ok = jnp.arange(LIST, dtype=jnp.int32) < listed_count
    own_block = block_ids == query_block
    positions = jnp.arange(MASK_BLOCK_SIZE, dtype=jnp.int32)
    causal = (positions[None, :] <= positions[:, None]) & (query_segs[None, :] == query_segs[:, None])
    earlier = block_ids < query_block
    return slot_ok[None, :, None] & jnp.where(own_block[None, :, None], causal[:, None, :], earlier[None, :, None])

def round_half(value_tensor):
    return lax.optimization_barrier(value_tensor.astype(jnp.bfloat16)).astype(jnp.float32)

def one_micro(operands):
    micro_queries, micro_keys, micro_values, micro_gradient, segs_m, lists_m, counts_m = operands
    heads_per_group = QUERY_HEADS // KEY_VALUE_HEADS
    scale_factor = 1.0 / math.sqrt(HEAD_SIZE)
    blocked_keys = micro_keys.reshape(QUERY_BLOCKS, MASK_BLOCK_SIZE, KEY_VALUE_HEADS, HEAD_SIZE)
    blocked_values = micro_values.reshape(QUERY_BLOCKS, MASK_BLOCK_SIZE, KEY_VALUE_HEADS, HEAD_SIZE)
    highest = lax.Precision.HIGHEST

    def step(running_total, inputs):
        query_block, block_ids, listed_count = inputs
        first_row_index = (query_block * MASK_BLOCK_SIZE).astype(jnp.int32)
        query_row_slice = lax.dynamic_slice_in_dim(micro_queries, first_row_index, MASK_BLOCK_SIZE, 0).astype(jnp.float32).reshape(MASK_BLOCK_SIZE, KEY_VALUE_HEADS, heads_per_group, HEAD_SIZE)
        gradient_row_slice = lax.dynamic_slice_in_dim(micro_gradient, first_row_index, MASK_BLOCK_SIZE, 0).astype(jnp.float32).reshape(MASK_BLOCK_SIZE, KEY_VALUE_HEADS, heads_per_group, HEAD_SIZE)
        query_segs = lax.dynamic_slice_in_dim(segs_m, first_row_index, MASK_BLOCK_SIZE, 0)
        allowed = allowed_mask(block_ids, listed_count, query_block, query_segs)[None, None]
        listed_k = blocked_keys[block_ids].astype(jnp.float32)
        listed_v = blocked_values[block_ids].astype(jnp.float32)
        scores = jnp.einsum('igrd,ljgd->grilj', query_row_slice, listed_k, precision=highest) * scale_factor
        scores = jnp.where(allowed, scores, NEG_FILL)
        largest = lax.optimization_barrier(jnp.max(scores, axis=(3, 4), keepdims=True))
        weights = jnp.where(allowed, jnp.exp(scores - largest), 0.0)
        probs_full = weights / lax.optimization_barrier(jnp.sum(weights, axis=(3, 4), keepdims=True))
        dprobs = jnp.einsum('igrd,ljgd->grilj', gradient_row_slice, listed_v, precision=highest)
        row_delta = lax.optimization_barrier(jnp.sum(probs_full * dprobs, axis=(3, 4), keepdims=True))
        dscores = round_half(probs_full * (dprobs - row_delta))
        probs_half = round_half(probs_full)
        query_grad = jnp.einsum('grilj,ljgd->igrd', dscores, listed_k, precision=highest) * scale_factor
        key_grad = jnp.einsum('grilj,igrd->ljgd', dscores, query_row_slice, precision=highest) * scale_factor
        value_grad = jnp.einsum('grilj,igrd->ljgd', probs_half, gradient_row_slice, precision=highest)
        running_total = (running_total[0].at[block_ids].add(key_grad), running_total[1].at[block_ids].add(value_grad))
        return (running_total, query_grad.reshape(MASK_BLOCK_SIZE, QUERY_HEADS * HEAD_SIZE).astype(jnp.bfloat16))
    zeroed_total = jnp.zeros((QUERY_BLOCKS, MASK_BLOCK_SIZE, KEY_VALUE_HEADS, HEAD_SIZE), jnp.float32)
    inputs = (jnp.arange(QUERY_BLOCKS, dtype=jnp.int32), lists_m, counts_m)
    running_total, query_gradient_rows = lax.scan(step, (zeroed_total, zeroed_total), inputs)
    return (query_gradient_rows.reshape(MICRO_POSITIONS, QUERY_HEADS * HEAD_SIZE), running_total[0].reshape(MICRO_POSITIONS, KEY_VALUE_HEADS * HEAD_SIZE).astype(jnp.bfloat16), running_total[1].reshape(MICRO_POSITIONS, KEY_VALUE_HEADS * HEAD_SIZE).astype(jnp.bfloat16))

def reference(queries, key_heads, value_per_head, out_grads, segment_ids, block_lists, list_counts):
    query_gradient_rows, key_grads, value_grads = lax.map(one_micro, (queries, key_heads, value_per_head, out_grads, segment_ids, block_lists, list_counts))
    return (jnp.roll(query_gradient_rows, -1, axis=0), jnp.roll(key_grads, -1, axis=0), jnp.roll(value_grads, -1, axis=0))
```

```python
import functools
import math

import jax
import jax.numpy as jnp
from jax import lax
from jax.experimental import pallas as pl
from jax.experimental.pallas import tpu as pltpu
from jax.sharding import PartitionSpec as P

QUERY_HEADS = 32
GROUPS = 4
HEAD = 128
BLOCK = 128
LIST = 4
PER_GROUP = QUERY_HEADS // GROUPS
GROUP_WIDTH = PER_GROUP * HEAD
ROWS = 4
COLS = 4
NEG_FILL = -1e30
SCALE = 1.0 / math.sqrt(HEAD)
EXP2_SCALE = SCALE * math.log2(math.e)
MESH = pl.DeviceIdType.MESH


def body(
    lists, counts, segs, keys, values, queries, grads,
    dq_out, dk_out, dv_out,
    row0, row1, row2, row3, far0, far1, far2, far3,
    id_tile, id_in, id_smem,
    q_buf, g_buf, stage, mask0, kc, vc, kt, dk_acc, dv_acc, dq_buf,
    y_send, y_in, row_acc, l_send, l_in, r_send, r_in, fin,
    id_ss, id_rs, id_ls, qg_s,
    zs, zr, ys, yr, bs, br, rys, ryr, ls, lr, rs, rr, dqs, dqr, dks, dkr,
):
    rowkv = (row0, row1, row2, row3)
    far = (far0, far1, far2, far3)
    sec = lax.axis_index("section")
    blk = lax.axis_index("blk")
    sections = lax.axis_size("section")
    y = blk // COLS
    z = lax.rem(blk, COLS)

    def at(yy, zz):
        return (sec, yy * COLS + zz)

    def remote(src, dst, ssem, rsem, dev):
        return pltpu.make_async_remote_copy(
            src_ref=src, dst_ref=dst, send_sem=ssem, recv_sem=rsem,
            device_id=dev, device_id_type=MESH,
        )

    here = (sec, blk)
    behind = (lax.rem(sec + sections - 1, sections), blk)
    ahead = (lax.rem(sec + 1, sections), blk)

    q_copy = pltpu.make_async_copy(queries.at[0], q_buf, qg_s.at[0])
    g_copy = pltpu.make_async_copy(grads.at[0], g_buf, qg_s.at[1])
    q_copy.start()
    g_copy.start()

    barrier = pltpu.get_barrier_semaphore()
    peers = [behind, ahead]
    for d in (1, 3):
        peers.append(at(y, lax.rem(z + d, COLS)))
    for d in (1, 2, 3):
        peers.append(at(lax.rem(y + d, ROWS), z))
    for p in peers:
        pl.semaphore_signal(barrier, inc=1, device_id=p, device_id_type=MESH)

    lanes = lax.broadcasted_iota(jnp.int32, (8, BLOCK), 0)
    tile = jnp.zeros((8, BLOCK), jnp.int32)
    for s in range(LIST):
        tile = jnp.where(lanes == s, lists[s], tile)
    id_tile[...] = tile
    for g in range(GROUPS):
        for zz in range(COLS):
            @pl.when(z == zz)
            def _(g=g, zz=zz):
                rowkv[g][zz, :BLOCK] = keys[0, :, g * HEAD:(g + 1) * HEAD]
                rowkv[g][zz, BLOCK:] = values[0, :, g * HEAD:(g + 1) * HEAD]

    pl.semaphore_wait(barrier, len(peers))

    for lo in range(ROWS - 1):
        @pl.when(lo < y)
        def _(lo=lo):
            remote(id_tile, id_in.at[y], id_ss.at[lo], id_rs.at[y], at(lo, z)).start()

    def hop(g, src, to):
        return remote(rowkv[g].at[src], rowkv[g].at[src], zs.at[g, src, to], zr.at[g, src],
                      at(y, z + 1) if to else at(y, z - 1))

    for g in range(GROUPS):
        for zz in range(COLS):
            @pl.when(z == zz)
            def _(g=g, zz=zz):
                if zz < COLS - 1:
                    hop(g, zz, 1).start()
                if zz > 0:
                    hop(g, zz, 0).start()

    seg_row = jnp.broadcast_to(segs[...].astype(jnp.float32), (BLOCK, BLOCK))
    seg_col = seg_row.T
    key_pos = lax.broadcasted_iota(jnp.int32, (BLOCK, BLOCK), 0)
    query_pos = lax.broadcasted_iota(jnp.int32, (BLOCK, BLOCK), 1)
    mask0[...] = jnp.where((key_pos <= query_pos) & (seg_row == seg_col), 1.0, 0.0)

    for hi in range(1, ROWS):
        @pl.when(hi > y)
        def _(hi=hi):
            remote(id_tile, id_in.at[hi], id_ss.at[0], id_rs.at[hi], here).wait_recv()
            c = pltpu.make_async_copy(id_in.at[hi], id_smem.at[hi], id_ls.at[hi])
            c.start()
            c.wait()

    own_id = [lists[s] for s in range(LIST)]
    count = counts[0]

    def gather_row(g):
        for zz in range(COLS):
            @pl.when(z == zz)
            def _(zz=zz):
                for dist in range(1, COLS):
                    for src, onward in ((zz - dist, 1), (zz + dist, 0)):
                        if 0 <= src < COLS:
                            hop(g, src, onward).wait_recv()
                            if onward and zz < COLS - 1 or not onward and zz > 0:
                                hop(g, src, onward).start()

    def far_copy(g, lo, hi):
        return remote(stage.at[g, hi - 1], far[g].at[lo, pl.ds(1, 2)], ys.at[g, lo, hi - 1],
                      yr.at[g, lo], at(hi, z))

    def first_copy(g, hi):
        return remote(rowkv[g].at[0], far[g].at[0, 0], bs.at[g, hi - 1], br.at[g], at(hi, z))

    def send_listed(g):
        @pl.when(y == 0)
        def _():
            for hi in range(1, ROWS):
                first_copy(g, hi).start()
        for lo in range(ROWS - 1):
            @pl.when(y == lo)
            def _(lo=lo):
                for hi in sorted(range(lo + 1, ROWS), reverse=True):
                    for s in (2, 3):
                        idx = lax.rem(id_smem[hi, s, 0], COLS)
                        stage[g, hi - 1, s - 2] = rowkv[g][idx]
                    far_copy(g, lo, hi).start()

    def pick(g, s):
        block = own_id[s]
        r, c = block // COLS, lax.rem(block, COLS)
        near = rowkv[g][c]
        away = far[g][jnp.minimum(r, ROWS - 2), s - 1]
        return jnp.where(r == y, near, away)

    def y_copy(g, lo, hi):
        src, dst = (y_send.at[g], y_in.at[g, hi - 1]) if lo == 0 else (
            y_send.at[g, pl.ds(1, 2)], y_in.at[g, hi - 1, pl.ds(1, 2)])
        return remote(src, dst, rys.at[g, lo], ryr.at[g, hi - 1], at(lo, z))

    def dq_copy(g):
        cols = pl.ds(g * GROUP_WIDTH, GROUP_WIDTH)
        return remote(dq_buf.at[:, cols], dq_out.at[0, :, cols], dqs.at[g], dqr.at[g], behind)

    def compute(g):
        for lo in range(ROWS - 1):
            @pl.when(lo < y)
            def _(lo=lo):
                far_copy(g, lo, lo + 1).wait_recv()
        @pl.when(y > 0)
        def _():
            first_copy(g, 1).wait_recv()
        for s in range(LIST):
            if s == 0:
                both = rowkv[g][z]
            else:
                both = pick(g, s)
            kc[s * BLOCK:(s + 1) * BLOCK] = both[:BLOCK]
            vc[s * BLOCK:(s + 1) * BLOCK] = both[BLOCK:]
        kt[...] = kc[...].T
        dk_acc[...] = jnp.zeros_like(dk_acc)
        dv_acc[...] = jnp.zeros_like(dv_acc)
        diag = mask0[...] > 0.0
        diag2 = jnp.concatenate([diag, diag], axis=1)
        open_slot = [None] + [
            jnp.where((s < count) & (own_id[s] < blk), 0.0, NEG_FILL) for s in range(1, LIST)
        ]

        @pl.loop(0, PER_GROUP // 2)
        def _(pair):
            lo = pl.multiple_of(g * GROUP_WIDTH + pair * 2 * HEAD, HEAD)
            first, second = pl.ds(lo, HEAD), pl.ds(pl.multiple_of(lo + HEAD, HEAD), HEAD)
            qp = jnp.concatenate([q_buf[:, first], q_buf[:, second]], axis=0)
            gp = jnp.concatenate([g_buf[:, first], g_buf[:, second]], axis=0)
            nt = (((1,), (1,)), ((), ()))
            s_all = lax.dot_general(kc[...], qp, nt, preferred_element_type=jnp.float32) * EXP2_SCALE
            dp = lax.dot_general(vc[...], gp, nt, preferred_element_type=jnp.float32)
            parts = [jnp.where(diag2, s_all[:BLOCK], NEG_FILL)]
            for s in range(1, LIST):
                parts.append(s_all[s * BLOCK:(s + 1) * BLOCK] + open_slot[s])
            s_all = jnp.concatenate(parts, axis=0)
            top = jnp.max(s_all, axis=0, keepdims=True)
            w = jnp.exp2(s_all - top)
            p = w * (1.0 / jnp.sum(w, axis=0, keepdims=True))
            delta = jnp.sum(p * dp, axis=0, keepdims=True)
            ds = (p * (dp - delta)).astype(jnp.bfloat16)
            ph = p.astype(jnp.bfloat16)
            dk_acc[...] += jnp.dot(ds, qp, preferred_element_type=jnp.float32)
            dv_acc[...] += jnp.dot(ph, gp, preferred_element_type=jnp.float32)
            dqt = jnp.dot(kt[...], ds, preferred_element_type=jnp.float32) * SCALE
            dq = dqt.T.astype(jnp.bfloat16)
            dq_buf[:, first] = dq[:BLOCK]
            dq_buf[:, second] = dq[BLOCK:]

        dq_copy(g).start()
        for s in range(1, LIST):
            rows = slice(s * BLOCK, (s + 1) * BLOCK)
            y_send[g, s - 1, :BLOCK] = (dk_acc[rows] * SCALE).astype(jnp.bfloat16)
            y_send[g, s - 1, BLOCK:] = dv_acc[rows].astype(jnp.bfloat16)
        for hi in range(1, ROWS):
            @pl.when(y == hi)
            def _(hi=hi):
                for lo in range(hi):
                    y_copy(g, lo, hi).start()
        for t in range(COLS):
            this = y * COLS + t
            for half, (acc, factor) in enumerate(((dk_acc, SCALE), (dv_acc, 1.0))):
                total = jnp.zeros((BLOCK, HEAD), jnp.float32)
                for s in range(LIST):
                    total += jnp.where(own_id[s] == this, acc[s * BLOCK:(s + 1) * BLOCK], 0.0)
                row_acc[g, t, half * BLOCK:(half + 1) * BLOCK] = total * factor

    def add_rows(g):
        for hi in range(1, ROWS):
            @pl.when(hi > y)
            def _(hi=hi):
                @pl.when(y == 0)
                def _():
                    y_copy(g, 0, hi).wait_recv()
                @pl.when(y > 0)
                def _():
                    y_copy(g, 1, hi).wait_recv()
                for t in range(COLS):
                    total = row_acc[g, t]
                    for s in (2, 3):
                        hit = id_smem[hi, s, 0] == y * COLS + t
                        total += jnp.where(hit, y_in[g, hi - 1, s - 1].astype(jnp.float32), 0.0)
                    row_acc[g, t] = total
                @pl.when(y == 0)
                def _():
                    row_acc[g, 0] += y_in[g, hi - 1, 0].astype(jnp.float32)

    def l_copy(g, t):
        return remote(l_send.at[g, t], l_in.at[g, t], ls.at[g, t], lr.at[g, t], at(y, z - 1))

    def r_copy(g, t):
        return remote(r_send.at[g, t], r_in.at[g, t], rs.at[g, t], rr.at[g, t], at(y, z + 1))

    def reduce_row(g, step):
        for zz in range(COLS):
            @pl.when(z == zz)
            def _(zz=zz):
                if zz == COLS - 1 - step:
                    for t in range(zz):
                        total = row_acc[g, t]
                        if step > 0:
                            l_copy(g, t).wait_recv()
                            total += l_in[g, t].astype(jnp.float32)
                        l_send[g, t] = total.astype(jnp.bfloat16)
                        l_copy(g, t).start()
                if zz == step:
                    for t in range(COLS - 1, zz, -1):
                        total = row_acc[g, t]
                        if step > 0:
                            r_copy(g, t).wait_recv()
                            total += r_in[g, t].astype(jnp.float32)
                        r_send[g, t] = total.astype(jnp.bfloat16)
                        r_copy(g, t).start()

    def out_copies(g):
        cols = pl.ds(g * HEAD, HEAD)
        return (
            remote(fin.at[g, pl.ds(0, BLOCK)], dk_out.at[0, :, cols], dks.at[g, 0], dkr.at[g, 0], behind),
            remote(fin.at[g, pl.ds(BLOCK, BLOCK)], dv_out.at[0, :, cols], dks.at[g, 1], dkr.at[g, 1], behind),
        )

    def finish(g):
        for zz in range(COLS):
            @pl.when(z == zz)
            def _(zz=zz):
                total = row_acc[g, zz]
                if zz < COLS - 1:
                    l_copy(g, zz).wait_recv()
                    total += l_in[g, zz].astype(jnp.float32)
                if zz > 0:
                    r_copy(g, zz).wait_recv()
                    total += r_in[g, zz].astype(jnp.float32)
                fin[g] = total.astype(jnp.bfloat16)
        for c in out_copies(g):
            c.start()

    gather_row(0)
    send_listed(0)
    gather_row(1)
    send_listed(1)
    q_copy.wait()
    g_copy.wait()
    compute(0)
    gather_row(2)
    send_listed(2)
    compute(1)
    add_rows(0)
    reduce_row(0, 0)
    gather_row(3)
    send_listed(3)
    compute(2)
    reduce_row(0, 1)
    add_rows(1)
    reduce_row(1, 0)
    reduce_row(0, 2)
    compute(3)
    finish(0)
    reduce_row(1, 1)
    add_rows(2)
    reduce_row(2, 0)
    reduce_row(1, 2)
    reduce_row(2, 1)
    finish(1)
    reduce_row(2, 2)
    add_rows(3)
    reduce_row(3, 0)
    finish(2)
    reduce_row(3, 1)
    reduce_row(3, 2)
    finish(3)

    for g in range(GROUPS):
        dq_copy(g).wait()
        for c in out_copies(g):
            c.wait()
        for zz in range(COLS):
            @pl.when(z == zz)
            def _(g=g, zz=zz):
                for src in range(COLS):
                    if src <= zz < COLS - 1:
                        hop(g, src, 1).wait_send()
                    if src >= zz > 0:
                        hop(g, src, 0).wait_send()
                for t in range(zz):
                    l_copy(g, t).wait_send()
                for t in range(zz + 1, COLS):
                    r_copy(g, t).wait_send()
        for yy in range(ROWS):
            @pl.when(y == yy)
            def _(g=g, yy=yy):
                for hi in range(yy + 1, ROWS):
                    far_copy(g, yy, hi).wait_send()
                    if yy == 0:
                        first_copy(g, hi).wait_send()
                for lo in range(yy):
                    y_copy(g, lo, yy).wait_send()
    for lo in range(ROWS - 1):
        @pl.when(lo < y)
        def _(lo=lo):
            remote(id_tile, id_in.at[y], id_ss.at[lo], id_rs.at[y], at(lo, z)).wait_send()


def per_device(queries, key_heads, value_per_head, out_grads, segment_ids, block_lists, list_counts):
    bf, f32 = jnp.bfloat16, jnp.float32
    anywhere = pl.BlockSpec(memory_space=pl.ANY)
    vmem = pl.BlockSpec(memory_space=pltpu.VMEM)
    smem = pl.BlockSpec(memory_space=pltpu.SMEM)
    two = 2 * BLOCK
    dma = pltpu.SemaphoreType.DMA
    keys_n = LIST * BLOCK
    scratch = (
        [pltpu.VMEM((COLS, two, HEAD), bf)] * GROUPS
        + [pltpu.VMEM((ROWS - 1, 3, two, HEAD), bf)] * GROUPS
        + [
            pltpu.VMEM((8, BLOCK), jnp.int32),
            pltpu.VMEM((ROWS, 8, BLOCK), jnp.int32),
            pltpu.SMEM((ROWS, 8, BLOCK), jnp.int32),
            pltpu.VMEM((BLOCK, QUERY_HEADS * HEAD), bf),
            pltpu.VMEM((BLOCK, QUERY_HEADS * HEAD), bf),
            pltpu.VMEM((GROUPS, ROWS - 1, 2, two, HEAD), bf),
            pltpu.VMEM((BLOCK, BLOCK), f32),
            pltpu.VMEM((keys_n, HEAD), bf),
            pltpu.VMEM((keys_n, HEAD), bf),
            pltpu.VMEM((HEAD, keys_n), bf),
            pltpu.VMEM((keys_n, HEAD), f32),
            pltpu.VMEM((keys_n, HEAD), f32),
            pltpu.VMEM((BLOCK, QUERY_HEADS * HEAD), bf),
            pltpu.VMEM((GROUPS, 3, two, HEAD), bf),
            pltpu.VMEM((GROUPS, ROWS - 1, 3, two, HEAD), bf),
            pltpu.VMEM((GROUPS, COLS, two, HEAD), f32),
            pltpu.VMEM((GROUPS, COLS, two, HEAD), bf),
            pltpu.VMEM((GROUPS, COLS, two, HEAD), bf),
            pltpu.VMEM((GROUPS, COLS, two, HEAD), bf),
            pltpu.VMEM((GROUPS, COLS, two, HEAD), bf),
            pltpu.VMEM((GROUPS, two, HEAD), bf),
            dma((ROWS,)), dma((ROWS,)), dma((ROWS,)), dma((2,)),
            dma((GROUPS, COLS, 2)), dma((GROUPS, COLS)),
            dma((GROUPS, ROWS, ROWS)), dma((GROUPS, ROWS)),
            dma((GROUPS, ROWS)), dma((GROUPS,)),
            dma((GROUPS, ROWS)), dma((GROUPS, ROWS)),
            dma((GROUPS, COLS)), dma((GROUPS, COLS)),
            dma((GROUPS, COLS)), dma((GROUPS, COLS)),
            dma((GROUPS,)), dma((GROUPS,)),
            dma((GROUPS, 2)), dma((GROUPS, 2)),
        ]
    )
    return pl.pallas_call(
        body,
        name="attention_grads",
        out_shape=(
            jax.ShapeDtypeStruct(queries.shape, bf),
            jax.ShapeDtypeStruct(key_heads.shape, bf),
            jax.ShapeDtypeStruct(value_per_head.shape, bf),
        ),
        in_specs=[smem, smem, vmem, vmem, vmem, anywhere, anywhere],
        out_specs=(anywhere, anywhere, anywhere),
        scratch_shapes=scratch,
        compiler_params=pltpu.CompilerParams(
            collective_id=0, has_side_effects=True, vmem_limit_bytes=48 << 20
        ),
    )(
        block_lists.reshape(LIST), list_counts.reshape(1), segment_ids,
        key_heads, value_per_head, queries, out_grads,
    )


def solution(mesh):
    rows = P("section", "blk", None)
    flat = P("section", "blk")
    return jax.shard_map(
        per_device,
        mesh=mesh,
        in_specs=(rows, rows, rows, rows, flat, rows, flat),
        out_specs=(rows, rows, rows),
        check_vma=False,
    )
```

```python
import functools
import math

import jax
import jax.numpy as jnp
from jax import lax
from jax.experimental import pallas as pl
from jax.experimental.pallas import tpu as pltpu
from jax.sharding import PartitionSpec as P

QUERY_HEADS = 32
GROUPS = 4
HEAD = 128
BLOCK = 128
LIST = 4
PER_GROUP = QUERY_HEADS // GROUPS
GROUP_WIDTH = PER_GROUP * HEAD
ROWS = 4
COLS = 4
NEG_FILL = -1e30
SCALE = 1.0 / math.sqrt(HEAD)
EXP2_SCALE = SCALE * math.log2(math.e)
MESH = pl.DeviceIdType.MESH


def body(
    lists, counts, segs, keys, values, queries, grads,
    dq_out, dk_out, dv_out,
    row0, row1, row2, row3, far0, far1, far2, far3,
    id_tile, id_in, id_smem,
    q_buf, g_buf, stage, mask0, kc, vc, kt, dk_acc, dv_acc, dq_buf,
    y_send, y_in, row_acc, z_send, z_in, fin, transit,
    id_ss, id_rs, id_ls, qg_s, kv_s,
    zs, zr, ys, yr, bs, br, rys, ryr, rzs, rzr, dqs, dqr, dks, dkr, trs, trr, tfs,
):
    rowkv = (row0, row1, row2, row3)
    far = (far0, far1, far2, far3)
    sec = lax.axis_index("section")
    blk = lax.axis_index("blk")
    sections = lax.axis_size("section")
    y = blk // COLS
    z = lax.rem(blk, COLS)

    def at(yy, zz):
        return (sec, yy * COLS + zz)

    def remote(src, dst, ssem, rsem, dev):
        return pltpu.make_async_remote_copy(
            src_ref=src, dst_ref=dst, send_sem=ssem, recv_sem=rsem,
            device_id=dev, device_id_type=MESH,
        )

    here = (sec, blk)
    behind = (lax.rem(sec + sections - 1, sections), blk)
    ahead = (lax.rem(sec + 1, sections), blk)

    half = sec // 8
    x = lax.rem(sec, 8) // 2
    core = lax.rem(sec, 2)
    wraps = lax.rem(sec, 8) == 0
    relays = (core == 1) & (x > 0)
    lands = (core == 1) & (x == 3)
    relay_from = (half * 8, blk)
    relay_to = (lax.rem(half + 1, 2) * 8 + 7, blk)

    def relay_at(q):
        return (half * 8 + 2 * q + 1, blk)

    own_kv = []
    for g in range(GROUPS):
        cols = pl.ds(g * HEAD, HEAD)
        own_kv.append(pltpu.make_async_copy(keys.at[0, :, cols], rowkv[g].at[z, pl.ds(0, BLOCK)], kv_s.at[g, 0]))
        own_kv.append(pltpu.make_async_copy(values.at[0, :, cols], rowkv[g].at[z, pl.ds(BLOCK, BLOCK)], kv_s.at[g, 1]))
    for c in own_kv:
        c.start()

    q_copy = pltpu.make_async_copy(queries.at[0], q_buf, qg_s.at[0])
    g_copy = pltpu.make_async_copy(grads.at[0], g_buf, qg_s.at[1])
    q_copy.start()
    g_copy.start()

    barrier = pltpu.get_barrier_semaphore()
    peers = [behind, ahead]
    for d in (1, 2, 3):
        peers.append(at(y, lax.rem(z + d, COLS)))
    for d in (1, 2, 3):
        peers.append(at(lax.rem(y + d, ROWS), z))
    for p in peers:
        pl.semaphore_signal(barrier, inc=1, device_id=p, device_id_type=MESH)

    @pl.when(wraps)
    def _():
        for q in range(1, ROWS):
            pl.semaphore_signal(barrier, inc=1, device_id=relay_at(q), device_id_type=MESH)

    @pl.when(relays)
    def _():
        pl.semaphore_signal(barrier, inc=1, device_id=relay_from, device_id_type=MESH)
        pl.semaphore_signal(barrier, inc=1, device_id=relay_to, device_id_type=MESH)

    @pl.when(lands)
    def _():
        for q in range(1, ROWS):
            other = (lax.rem(half + 1, 2) * 8 + 2 * q + 1, blk)
            pl.semaphore_signal(barrier, inc=1, device_id=other, device_id_type=MESH)

    lanes = lax.broadcasted_iota(jnp.int32, (8, BLOCK), 0)
    tile = jnp.zeros((8, BLOCK), jnp.int32)
    for s in range(LIST):
        tile = jnp.where(lanes == s, lists[s], tile)
    id_tile[...] = tile
    for c in own_kv:
        c.wait()
    greeted = len(peers) + jnp.where(wraps | lands, 3, 0) + jnp.where(relays, 2, 0)
    pl.semaphore_wait(barrier, greeted)

    for lo in range(ROWS - 1):
        @pl.when(lo < y)
        def _(lo=lo):
            remote(id_tile, id_in.at[y], id_ss.at[lo], id_rs.at[y], at(lo, z)).start()

    def row_copy(g, d):
        return remote(rowkv[g].at[z], rowkv[g].at[z], zs.at[g, d], zr.at[g, d],
                      at(y, lax.rem(z + d, COLS)))

    def start_row(g):
        for d in range(1, COLS):
            row_copy(g, d).start()

    start_row(0)

    seg_row = jnp.broadcast_to(segs[...].astype(jnp.float32), (BLOCK, BLOCK))
    seg_col = seg_row.T
    key_pos = lax.broadcasted_iota(jnp.int32, (BLOCK, BLOCK), 0)
    query_pos = lax.broadcasted_iota(jnp.int32, (BLOCK, BLOCK), 1)
    mask0[...] = jnp.where((key_pos <= query_pos) & (seg_row == seg_col), 1.0, 0.0)

    def read_lists():
        copies = {hi: pltpu.make_async_copy(id_in.at[hi], id_smem.at[hi], id_ls.at[hi]) for hi in range(1, ROWS)}
        for hi in range(1, ROWS):
            @pl.when(hi > y)
            def _(hi=hi):
                remote(id_tile, id_in.at[hi], id_ss.at[0], id_rs.at[hi], here).wait_recv()
                copies[hi].start()
        for hi in range(1, ROWS):
            @pl.when(hi > y)
            def _(hi=hi):
                copies[hi].wait()

    own_id = [lists[s] for s in range(LIST)]
    count = counts[0]

    def gather_row(g):
        for d in range(1, COLS):
            row_copy(g, d).wait_recv()
        if g + 1 < GROUPS:
            start_row(g + 1)

    def far_copy(g, lo, hi):
        return remote(stage.at[g, hi - 1], far[g].at[lo, pl.ds(1, 2)], ys.at[g, lo, hi - 1],
                      yr.at[g, lo], at(hi, z))

    def first_copy(g, hi):
        return remote(rowkv[g].at[0], far[g].at[0, 0], bs.at[g, hi - 1], br.at[g], at(hi, z))

    def send_listed(g):
        @pl.when(y == 0)
        def _():
            for hi in range(1, ROWS):
                first_copy(g, hi).start()
        for lo in range(ROWS - 1):
            @pl.when(y == lo)
            def _(lo=lo):
                for hi in sorted(range(lo + 1, ROWS), reverse=True):
                    for s in (2, 3):
                        idx = lax.rem(id_smem[hi, s, 0], COLS)
                        stage[g, hi - 1, s - 2] = rowkv[g][idx]
                    far_copy(g, lo, hi).start()

    def pick(g, s):
        block = own_id[s]
        r, c = block // COLS, lax.rem(block, COLS)
        near = rowkv[g][c]
        away = far[g][jnp.minimum(r, ROWS - 2), s - 1]
        return jnp.where(r == y, near, away)

    def y_copy(g, lo, hi):
        src, dst = (y_send.at[g], y_in.at[g, hi - 1]) if lo == 0 else (
            y_send.at[g, pl.ds(1, 2)], y_in.at[g, hi - 1, pl.ds(1, 2)])
        return remote(src, dst, rys.at[g, lo], ryr.at[g, hi - 1], at(lo, z))

    def dq_copy(g, q, dev):
        part = (pl.ds(q * 32, 32), pl.ds(g * GROUP_WIDTH, GROUP_WIDTH))
        return remote(dq_buf.at[part], dq_out.at[(0,) + part], dqs.at[g, q], dqr.at[g, q], dev)

    def spread_copy(g, q):
        part = (pl.ds(q * 32, 32), pl.ds(g * GROUP_WIDTH, GROUP_WIDTH))
        return remote(dq_buf.at[part], transit.at[g], dqs.at[g, q], trr.at[g], relay_at(q))

    def pass_copy(g, q):
        part = (0, pl.ds(q * 32, 32), pl.ds(g * GROUP_WIDTH, GROUP_WIDTH))
        return remote(transit.at[g], dq_out.at[part], tfs.at[g], dqr.at[g, q], relay_to)

    def send_dq(g):
        dq_copy(g, 0, behind).start()
        for q in range(1, ROWS):
            @pl.when(wraps)
            def _(q=q):
                spread_copy(g, q).start()
            @pl.when(jnp.logical_not(wraps))
            def _(q=q):
                dq_copy(g, q, behind).start()

    def pass_on(g):
        for q in range(1, ROWS):
            @pl.when(relays & (x == q))
            def _(q=q):
                spread_copy(g, q).wait_recv()
                pass_copy(g, q).start()

    def compute(g):
        for lo in range(ROWS - 1):
            @pl.when(lo < y)
            def _(lo=lo):
                far_copy(g, lo, lo + 1).wait_recv()
        @pl.when(y > 0)
        def _():
            first_copy(g, 1).wait_recv()
        for s in range(LIST):
            if s == 0:
                both = rowkv[g][z]
            else:
                both = pick(g, s)
            kc[s * BLOCK:(s + 1) * BLOCK] = both[:BLOCK]
            vc[s * BLOCK:(s + 1) * BLOCK] = both[BLOCK:]
        kt[...] = kc[...].T
        dk_acc[...] = jnp.zeros_like(dk_acc)
        dv_acc[...] = jnp.zeros_like(dv_acc)
        diag = mask0[...] > 0.0
        diag2 = jnp.concatenate([diag, diag], axis=1)
        open_slot = [None] + [
            jnp.where((s < count) & (own_id[s] < blk), 0.0, NEG_FILL) for s in range(1, LIST)
        ]

        @pl.loop(0, PER_GROUP // 2)
        def _(pair):
            lo = pl.multiple_of(g * GROUP_WIDTH + pair * 2 * HEAD, HEAD)
            first, second = pl.ds(lo, HEAD), pl.ds(pl.multiple_of(lo + HEAD, HEAD), HEAD)
            qp = jnp.concatenate([q_buf[:, first], q_buf[:, second]], axis=0)
            gp = jnp.concatenate([g_buf[:, first], g_buf[:, second]], axis=0)
            nt = (((1,), (1,)), ((), ()))
            s_all = lax.dot_general(kc[...], qp, nt, preferred_element_type=jnp.float32) * EXP2_SCALE
            dp = lax.dot_general(vc[...], gp, nt, preferred_element_type=jnp.float32)
            parts = [jnp.where(diag2, s_all[:BLOCK], NEG_FILL)]
            for s in range(1, LIST):
                parts.append(s_all[s * BLOCK:(s + 1) * BLOCK] + open_slot[s])
            s_all = jnp.concatenate(parts, axis=0)
            top = jnp.max(s_all, axis=0, keepdims=True)
            w = jnp.exp2(s_all - top)
            p = w * (1.0 / jnp.sum(w, axis=0, keepdims=True))
            delta = jnp.sum(p * dp, axis=0, keepdims=True)
            ds = (p * (dp - delta)).astype(jnp.bfloat16)
            ph = p.astype(jnp.bfloat16)
            dk_acc[...] += jnp.dot(ds, qp, preferred_element_type=jnp.float32)
            dv_acc[...] += jnp.dot(ph, gp, preferred_element_type=jnp.float32)
            dqt = jnp.dot(kt[...], ds, preferred_element_type=jnp.float32) * SCALE
            dq = dqt.T.astype(jnp.bfloat16)
            dq_buf[:, first] = dq[:BLOCK]
            dq_buf[:, second] = dq[BLOCK:]

        send_dq(g)
        for s in range(1, LIST):
            rows = slice(s * BLOCK, (s + 1) * BLOCK)
            y_send[g, s - 1, :BLOCK] = (dk_acc[rows] * SCALE).astype(jnp.bfloat16)
            y_send[g, s - 1, BLOCK:] = dv_acc[rows].astype(jnp.bfloat16)
        for hi in range(1, ROWS):
            @pl.when(y == hi)
            def _(hi=hi):
                for lo in range(hi):
                    y_copy(g, lo, hi).start()
        for t in range(COLS):
            this = y * COLS + t
            for half, (acc, factor) in enumerate(((dk_acc, SCALE), (dv_acc, 1.0))):
                total = jnp.zeros((BLOCK, HEAD), jnp.float32)
                for s in range(LIST):
                    total += jnp.where(own_id[s] == this, acc[s * BLOCK:(s + 1) * BLOCK], 0.0)
                row_acc[g, t, half * BLOCK:(half + 1) * BLOCK] = total * factor

    def add_rows(g):
        for hi in range(1, ROWS):
            @pl.when(hi > y)
            def _(hi=hi):
                @pl.when(y == 0)
                def _():
                    y_copy(g, 0, hi).wait_recv()
                @pl.when(y > 0)
                def _():
                    y_copy(g, 1, hi).wait_recv()
                for t in range(COLS):
                    total = row_acc[g, t]
                    for s in (2, 3):
                        hit = id_smem[hi, s, 0] == y * COLS + t
                        total += jnp.where(hit, y_in[g, hi - 1, s - 1].astype(jnp.float32), 0.0)
                    row_acc[g, t] = total
                @pl.when(y == 0)
                def _():
                    row_acc[g, 0] += y_in[g, hi - 1, 0].astype(jnp.float32)

    def reduce_copy(g, d):
        return remote(z_send.at[g, d - 1], z_in.at[g, d - 1], rzs.at[g, d], rzr.at[g, d],
                      at(y, lax.rem(z + d, COLS)))

    def send_row(g):
        for d in range(1, COLS):
            z_send[g, d - 1] = row_acc[g, lax.rem(z + d, COLS)].astype(jnp.bfloat16)
            reduce_copy(g, d).start()

    def out_copies(g):
        cols = pl.ds(g * HEAD, HEAD)
        return (
            remote(fin.at[g, pl.ds(0, BLOCK)], dk_out.at[0, :, cols], dks.at[g, 0], dkr.at[g, 0], behind),
            remote(fin.at[g, pl.ds(BLOCK, BLOCK)], dv_out.at[0, :, cols], dks.at[g, 1], dkr.at[g, 1], behind),
        )

    def finish(g):
        total = row_acc[g, z]
        for d in range(1, COLS):
            reduce_copy(g, d).wait_recv()
            total += z_in[g, d - 1].astype(jnp.float32)
        fin[g] = total.astype(jnp.bfloat16)
        for c in out_copies(g):
            c.start()

    gather_row(0)
    read_lists()
    send_listed(0)
    gather_row(1)
    send_listed(1)
    q_copy.wait()
    g_copy.wait()
    compute(0)
    gather_row(2)
    send_listed(2)
    compute(1)
    gather_row(3)
    send_listed(3)
    pass_on(0)
    add_rows(0)
    send_row(0)
    compute(2)
    pass_on(1)
    add_rows(1)
    send_row(1)
    finish(0)
    compute(3)
    pass_on(2)
    add_rows(2)
    send_row(2)
    finish(1)
    pass_on(3)
    finish(2)
    add_rows(3)
    send_row(3)
    finish(3)

    for g in range(GROUPS):
        for q in range(ROWS):
            dq_copy(g, q, behind).wait()
        for q in range(1, ROWS):
            @pl.when(relays & (x == q))
            def _(g=g, q=q):
                pass_copy(g, q).wait_send()
        for c in out_copies(g):
            c.wait()
        for d in range(1, COLS):
            row_copy(g, d).wait_send()
            reduce_copy(g, d).wait_send()
        for yy in range(ROWS):
            @pl.when(y == yy)
            def _(g=g, yy=yy):
                for hi in range(yy + 1, ROWS):
                    far_copy(g, yy, hi).wait_send()
                    if yy == 0:
                        first_copy(g, hi).wait_send()
                for lo in range(yy):
                    y_copy(g, lo, yy).wait_send()
    for lo in range(ROWS - 1):
        @pl.when(lo < y)
        def _(lo=lo):
            remote(id_tile, id_in.at[y], id_ss.at[lo], id_rs.at[y], at(lo, z)).wait_send()


def per_device(queries, key_heads, value_per_head, out_grads, segment_ids, block_lists, list_counts):
    bf, f32 = jnp.bfloat16, jnp.float32
    anywhere = pl.BlockSpec(memory_space=pl.ANY)
    vmem = pl.BlockSpec(memory_space=pltpu.VMEM)
    smem = pl.BlockSpec(memory_space=pltpu.SMEM)
    two = 2 * BLOCK
    dma = pltpu.SemaphoreType.DMA
    keys_n = LIST * BLOCK
    scratch = (
        [pltpu.VMEM((COLS, two, HEAD), bf)] * GROUPS
        + [pltpu.VMEM((ROWS - 1, 3, two, HEAD), bf)] * GROUPS
        + [
            pltpu.VMEM((8, BLOCK), jnp.int32),
            pltpu.VMEM((ROWS, 8, BLOCK), jnp.int32),
            pltpu.SMEM((ROWS, 8, BLOCK), jnp.int32),
            pltpu.VMEM((BLOCK, QUERY_HEADS * HEAD), bf),
            pltpu.VMEM((BLOCK, QUERY_HEADS * HEAD), bf),
            pltpu.VMEM((GROUPS, ROWS - 1, 2, two, HEAD), bf),
            pltpu.VMEM((BLOCK, BLOCK), f32),
            pltpu.VMEM((keys_n, HEAD), bf),
            pltpu.VMEM((keys_n, HEAD), bf),
            pltpu.VMEM((HEAD, keys_n), bf),
            pltpu.VMEM((keys_n, HEAD), f32),
            pltpu.VMEM((keys_n, HEAD), f32),
            pltpu.VMEM((BLOCK, QUERY_HEADS * HEAD), bf),
            pltpu.VMEM((GROUPS, 3, two, HEAD), bf),
            pltpu.VMEM((GROUPS, ROWS - 1, 3, two, HEAD), bf),
            pltpu.VMEM((GROUPS, COLS, two, HEAD), f32),
            pltpu.VMEM((GROUPS, COLS - 1, two, HEAD), bf),
            pltpu.VMEM((GROUPS, COLS - 1, two, HEAD), bf),
            pltpu.VMEM((GROUPS, two, HEAD), bf),
            pltpu.VMEM((GROUPS, BLOCK // 4, GROUP_WIDTH), bf),
            dma((ROWS,)), dma((ROWS,)), dma((ROWS,)), dma((2,)), dma((GROUPS, 2)),
            dma((GROUPS, COLS)), dma((GROUPS, COLS)),
            dma((GROUPS, ROWS, ROWS)), dma((GROUPS, ROWS)),
            dma((GROUPS, ROWS)), dma((GROUPS,)),
            dma((GROUPS, ROWS)), dma((GROUPS, ROWS)),
            dma((GROUPS, COLS)), dma((GROUPS, COLS)),
            dma((GROUPS, 4)), dma((GROUPS, 4)),
            dma((GROUPS, 2)), dma((GROUPS, 2)),
            dma((GROUPS,)), dma((GROUPS,)), dma((GROUPS,)),
        ]
    )
    return pl.pallas_call(
        body,
        name="attention_grads",
        out_shape=(
            jax.ShapeDtypeStruct(queries.shape, bf),
            jax.ShapeDtypeStruct(key_heads.shape, bf),
            jax.ShapeDtypeStruct(value_per_head.shape, bf),
        ),
        in_specs=[smem, smem, vmem, anywhere, anywhere, anywhere, anywhere],
        out_specs=(anywhere, anywhere, anywhere),
        scratch_shapes=scratch,
        compiler_params=pltpu.CompilerParams(
            collective_id=0, has_side_effects=True, vmem_limit_bytes=62 << 20
        ),
    )(
        block_lists.reshape(LIST), list_counts.reshape(1), segment_ids,
        key_heads, value_per_head, queries, out_grads,
    )


def solution(mesh):
    rows = P("section", "blk", None)
    flat = P("section", "blk")
    return jax.shard_map(
        per_device,
        mesh=mesh,
        in_specs=(rows, rows, rows, rows, flat, rows, flat),
        out_specs=(rows, rows, rows),
        check_vma=False,
    )
```

```python
import functools
import math

import jax
import jax.numpy as jnp
from jax import lax
from jax.experimental import pallas as pl
from jax.experimental.pallas import tpu as pltpu
from jax.sharding import PartitionSpec as P

QUERY_HEADS = 32
GROUPS = 4
HEAD = 128
BLOCK = 128
LIST = 4
PER_GROUP = QUERY_HEADS // GROUPS
GROUP_WIDTH = PER_GROUP * HEAD
ROWS = 4
COLS = 4
NEG_FILL = -1e30
SCALE = 1.0 / math.sqrt(HEAD)
EXP2_SCALE = SCALE * math.log2(math.e)
MESH = pl.DeviceIdType.MESH


def body(
    lists, counts, segs, keys, values, queries, grads,
    dq_out, dk_out, dv_out,
    row0, row1, row2, row3, far0, far1, far2, far3,
    id_tile, id_in, id_smem,
    q_buf, g_buf, stage, mask0, kc, vc, kt, dk_acc, dv_acc, dq_buf,
    y_send, y_in, row_acc, z_send, z_in, fin, transit, lead_in, lead_out,
    id_ss, id_rs, id_ls, qg_s, kv_s,
    zs, zr, ys, yr, bs, br, rys, ryr, rzs, rzr, dqs, dqr, dks, dkr, trs, trr, tfs,
    lis, lir, los, lor,
):
    rowkv = (row0, row1, row2, row3)
    far = (far0, far1, far2, far3)
    sec = lax.axis_index("section")
    blk = lax.axis_index("blk")
    sections = lax.axis_size("section")
    y = blk // COLS
    z = lax.rem(blk, COLS)

    def at(yy, zz):
        return (sec, yy * COLS + zz)

    def remote(src, dst, ssem, rsem, dev):
        return pltpu.make_async_remote_copy(
            src_ref=src, dst_ref=dst, send_sem=ssem, recv_sem=rsem,
            device_id=dev, device_id_type=MESH,
        )

    here = (sec, blk)
    behind = (lax.rem(sec + sections - 1, sections), blk)
    ahead = (lax.rem(sec + 1, sections), blk)

    half = sec // 8
    x = lax.rem(sec, 8) // 2
    core = lax.rem(sec, 2)
    wraps = lax.rem(sec, 8) == 0
    relays = (core == 1) & (x > 0)
    lands = (core == 1) & (x == 3)
    relay_from = (half * 8, blk)
    relay_to = (lax.rem(half + 1, 2) * 8 + 7, blk)

    def relay_at(q):
        return (half * 8 + 2 * q + 1, blk)

    own_kv = []
    for g in range(GROUPS):
        cols = pl.ds(g * HEAD, HEAD)
        own_kv.append(pltpu.make_async_copy(keys.at[0, :, cols], rowkv[g].at[z, pl.ds(0, BLOCK)], kv_s.at[g, 0]))
        own_kv.append(pltpu.make_async_copy(values.at[0, :, cols], rowkv[g].at[z, pl.ds(BLOCK, BLOCK)], kv_s.at[g, 1]))
    for c in own_kv:
        c.start()

    q_copy = pltpu.make_async_copy(queries.at[0], q_buf, qg_s.at[0])
    g_copy = pltpu.make_async_copy(grads.at[0], g_buf, qg_s.at[1])
    q_copy.start()
    g_copy.start()

    barrier = pltpu.get_barrier_semaphore()
    peers = [behind, ahead]
    for d in (1, 2, 3):
        peers.append(at(y, lax.rem(z + d, COLS)))
    for d in (1, 2, 3):
        peers.append(at(lax.rem(y + d, ROWS), z))
    for p in peers:
        pl.semaphore_signal(barrier, inc=1, device_id=p, device_id_type=MESH)

    @pl.when(wraps)
    def _():
        for q in range(1, ROWS):
            pl.semaphore_signal(barrier, inc=1, device_id=relay_at(q), device_id_type=MESH)

    @pl.when(relays)
    def _():
        pl.semaphore_signal(barrier, inc=1, device_id=relay_from, device_id_type=MESH)
        pl.semaphore_signal(barrier, inc=1, device_id=relay_to, device_id_type=MESH)

    @pl.when(lands)
    def _():
        for q in range(1, ROWS):
            other = (lax.rem(half + 1, 2) * 8 + 2 * q + 1, blk)
            pl.semaphore_signal(barrier, inc=1, device_id=other, device_id_type=MESH)

    lanes = lax.broadcasted_iota(jnp.int32, (8, BLOCK), 0)
    tile = jnp.zeros((8, BLOCK), jnp.int32)
    for s in range(LIST):
        tile = jnp.where(lanes == s, lists[s], tile)
    id_tile[...] = tile
    for c in own_kv:
        c.wait()
    greeted = len(peers) + jnp.where(wraps | lands, 3, 0) + jnp.where(relays, 2, 0)
    pl.semaphore_wait(barrier, greeted)

    for lo in range(ROWS - 1):
        @pl.when(lo < y)
        def _(lo=lo):
            remote(id_tile, id_in.at[y], id_ss.at[lo], id_rs.at[y], at(lo, z)).start()

    def row_copy(g, d):
        return remote(rowkv[g].at[z], rowkv[g].at[z], zs.at[g, d], zr.at[g, d],
                      at(y, lax.rem(z + d, COLS)))

    def start_row(g):
        for d in range(1, COLS):
            row_copy(g, d).start()

    start_row(0)

    seg_row = jnp.broadcast_to(segs[...].astype(jnp.float32), (BLOCK, BLOCK))
    seg_col = seg_row.T
    key_pos = lax.broadcasted_iota(jnp.int32, (BLOCK, BLOCK), 0)
    query_pos = lax.broadcasted_iota(jnp.int32, (BLOCK, BLOCK), 1)
    mask0[...] = jnp.where((key_pos <= query_pos) & (seg_row == seg_col), 1.0, 0.0)

    def read_lists():
        copies = {hi: pltpu.make_async_copy(id_in.at[hi], id_smem.at[hi], id_ls.at[hi]) for hi in range(1, ROWS)}
        for hi in range(1, ROWS):
            @pl.when(hi > y)
            def _(hi=hi):
                remote(id_tile, id_in.at[hi], id_ss.at[0], id_rs.at[hi], here).wait_recv()
                copies[hi].start()
        for hi in range(1, ROWS):
            @pl.when(hi > y)
            def _(hi=hi):
                copies[hi].wait()

    own_id = [lists[s] for s in range(LIST)]
    count = counts[0]

    def gather_row(g):
        for d in range(1, COLS):
            row_copy(g, d).wait_recv()
        if g + 1 < GROUPS:
            start_row(g + 1)

    def far_copy(g, lo, hi):
        return remote(stage.at[g, hi - 1], far[g].at[lo, pl.ds(1, 2)], ys.at[g, lo, hi - 1],
                      yr.at[g, lo], at(hi, z))

    def first_copy(g, hi):
        return remote(rowkv[g].at[0], far[g].at[0, 0], bs.at[g, hi - 1], br.at[g], at(hi, z))

    def hand_copy(g):
        return remote(far[g].at[0, 0], far[g].at[0, 0], bs.at[g, 1], br.at[g], at(2, z))

    def hand_first(g):
        @pl.when(y == 1)
        def _():
            first_copy(g, 1).wait_recv()
            hand_copy(g).start()

    def send_listed(g):
        @pl.when(y == 0)
        def _():
            for hi in (1, 3):
                first_copy(g, hi).start()
        for lo in range(ROWS - 1):
            @pl.when(y == lo)
            def _(lo=lo):
                for hi in sorted(range(lo + 1, ROWS), reverse=True):
                    for s in (2, 3):
                        idx = lax.rem(id_smem[hi, s, 0], COLS)
                        stage[g, hi - 1, s - 2] = rowkv[g][idx]
                    far_copy(g, lo, hi).start()

    def pick(g, s):
        block = own_id[s]
        r, c = block // COLS, lax.rem(block, COLS)
        near = rowkv[g][c]
        away = far[g][jnp.minimum(r, ROWS - 2), s - 1]
        return jnp.where(r == y, near, away)

    def direct(g, hi):
        return hi == 3

    def y_copy(g, lo, hi):
        src, dst = (y_send.at[g], y_in.at[g, hi - 1]) if lo == 0 and direct(g, hi) else (
            y_send.at[g, pl.ds(1, 2)], y_in.at[g, hi - 1, pl.ds(1, 2)])
        return remote(src, dst, rys.at[g, lo], ryr.at[g, hi - 1], at(lo, z))

    def lead_copy(g):
        return remote(y_send.at[g, 0], lead_in.at[g], lis.at[g], lir.at[g], at(1, z))

    def lead_end_copy(g):
        return remote(lead_out.at[g], y_in.at[g, 0, 0], los.at[g], lor.at[g], at(0, z))

    def fold_first(g):
        @pl.when(y == 1)
        def _():
            lead_copy(g).wait_recv()
            total = y_send[g, 0].astype(jnp.float32) + lead_in[g].astype(jnp.float32)
            lead_out[g] = total.astype(jnp.bfloat16)
            lead_end_copy(g).start()

    def dq_copy(g, q, dev):
        part = (pl.ds(q * 32, 32), pl.ds(g * GROUP_WIDTH, GROUP_WIDTH))
        return remote(dq_buf.at[part], dq_out.at[(0,) + part], dqs.at[g, q], dqr.at[g, q], dev)

    def spread_copy(g, q):
        part = (pl.ds(q * 32, 32), pl.ds(g * GROUP_WIDTH, GROUP_WIDTH))
        return remote(dq_buf.at[part], transit.at[g], dqs.at[g, q], trr.at[g], relay_at(q))

    def pass_copy(g, q):
        part = (0, pl.ds(q * 32, 32), pl.ds(g * GROUP_WIDTH, GROUP_WIDTH))
        return remote(transit.at[g], dq_out.at[part], tfs.at[g], dqr.at[g, q], relay_to)

    def whole_copy(g):
        cols = pl.ds(g * GROUP_WIDTH, GROUP_WIDTH)
        return remote(dq_buf.at[:, cols], dq_out.at[0, :, cols], dqs.at[g, 0], dqr.at[g, 0], behind)

    def send_dq(g):
        @pl.when(wraps)
        def _():
            for q in range(1, ROWS):
                spread_copy(g, q).start()
            dq_copy(g, 0, behind).start()

        @pl.when(jnp.logical_not(wraps))
        def _():
            whole_copy(g).start()

    def drain_dq(g):
        @pl.when(wraps)
        def _():
            for q in range(ROWS):
                dq_copy(g, q, behind).wait_send()

        @pl.when(jnp.logical_not(wraps))
        def _():
            whole_copy(g).wait_send()

        @pl.when(lands)
        def _():
            for q in range(ROWS):
                dq_copy(g, q, behind).wait_recv()

        @pl.when(jnp.logical_not(lands))
        def _():
            whole_copy(g).wait_recv()
        for q in range(1, ROWS):
            @pl.when(relays & (x == q))
            def _(q=q):
                pass_copy(g, q).wait_send()

    def pass_on(g):
        for q in range(1, ROWS):
            @pl.when(relays & (x == q))
            def _(q=q):
                spread_copy(g, q).wait_recv()
                pass_copy(g, q).start()

    def compute(g):
        for lo in range(ROWS - 1):
            @pl.when(lo < y)
            def _(lo=lo):
                far_copy(g, lo, lo + 1).wait_recv()
        @pl.when(y > 1)
        def _():
            first_copy(g, 1).wait_recv()
        for s in range(LIST):
            if s == 0:
                both = rowkv[g][z]
            else:
                both = pick(g, s)
            kc[s * BLOCK:(s + 1) * BLOCK] = both[:BLOCK]
            vc[s * BLOCK:(s + 1) * BLOCK] = both[BLOCK:]
        kt[...] = kc[...].T
        dk_acc[...] = jnp.zeros_like(dk_acc)
        dv_acc[...] = jnp.zeros_like(dv_acc)
        diag = mask0[...] > 0.0
        diag2 = jnp.concatenate([diag, diag], axis=1)
        open_slot = [None] + [
            jnp.where((s < count) & (own_id[s] < blk), 0.0, NEG_FILL) for s in range(1, LIST)
        ]

        @pl.loop(0, PER_GROUP // 2, unroll=True)
        def _(pair):
            lo = pl.multiple_of(g * GROUP_WIDTH + pair * 2 * HEAD, HEAD)
            first, second = pl.ds(lo, HEAD), pl.ds(pl.multiple_of(lo + HEAD, HEAD), HEAD)
            qp = jnp.concatenate([q_buf[:, first], q_buf[:, second]], axis=0)
            gp = jnp.concatenate([g_buf[:, first], g_buf[:, second]], axis=0)
            nt = (((1,), (1,)), ((), ()))
            s_all = lax.dot_general(kc[...], qp, nt, preferred_element_type=jnp.float32) * EXP2_SCALE
            dp = lax.dot_general(vc[...], gp, nt, preferred_element_type=jnp.float32)
            parts = [jnp.where(diag2, s_all[:BLOCK], NEG_FILL)]
            for s in range(1, LIST):
                parts.append(s_all[s * BLOCK:(s + 1) * BLOCK] + open_slot[s])
            s_all = jnp.concatenate(parts, axis=0)
            top = jnp.max(s_all, axis=0, keepdims=True)
            w = jnp.exp2(s_all - top)
            p = w * (1.0 / jnp.sum(w, axis=0, keepdims=True))
            delta = jnp.sum(p * dp, axis=0, keepdims=True)
            ds = (p * (dp - delta)).astype(jnp.bfloat16)
            ph = p.astype(jnp.bfloat16)
            dk_acc[...] += jnp.dot(ds, qp, preferred_element_type=jnp.float32)
            dv_acc[...] += jnp.dot(ph, gp, preferred_element_type=jnp.float32)
            dqt = jnp.dot(kt[...], ds, preferred_element_type=jnp.float32) * SCALE
            dq = dqt.T.astype(jnp.bfloat16)
            dq_buf[:, first] = dq[:BLOCK]
            dq_buf[:, second] = dq[BLOCK:]

        for s in range(1, LIST):
            rows = slice(s * BLOCK, (s + 1) * BLOCK)
            y_send[g, s - 1, :BLOCK] = (dk_acc[rows] * SCALE).astype(jnp.bfloat16)
            y_send[g, s - 1, BLOCK:] = dv_acc[rows].astype(jnp.bfloat16)
        for hi in range(1, ROWS):
            @pl.when(y == hi)
            def _(hi=hi):
                if hi == 2 and not direct(g, hi):
                    lead_copy(g).start()
                for lo in range(hi):
                    y_copy(g, lo, hi).start()
        send_dq(g)
        for t in range(COLS):
            this = y * COLS + t
            for half, (acc, factor) in enumerate(((dk_acc, SCALE), (dv_acc, 1.0))):
                total = jnp.zeros((BLOCK, HEAD), jnp.float32)
                for s in range(LIST):
                    total += jnp.where(own_id[s] == this, acc[s * BLOCK:(s + 1) * BLOCK], 0.0)
                row_acc[g, t, half * BLOCK:(half + 1) * BLOCK] = total * factor

    def add_rows(g):
        for hi in range(1, ROWS):
            @pl.when(hi > y)
            def _(hi=hi):
                @pl.when(y == 0)
                def _():
                    y_copy(g, 0, hi).wait_recv()
                    if hi == 1 and not direct(g, hi):
                        lead_end_copy(g).wait_recv()
                @pl.when(y > 0)
                def _():
                    y_copy(g, 1, hi).wait_recv()
                for t in range(COLS):
                    total = row_acc[g, t]
                    for s in (2, 3):
                        hit = id_smem[hi, s, 0] == y * COLS + t
                        total += jnp.where(hit, y_in[g, hi - 1, s - 1].astype(jnp.float32), 0.0)
                    row_acc[g, t] = total
                if hi != 2 or direct(g, hi):
                    @pl.when(y == 0)
                    def _():
                        row_acc[g, 0] += y_in[g, hi - 1, 0].astype(jnp.float32)

    def reduce_copy(g, d):
        return remote(z_send.at[g, d - 1], z_in.at[g, d - 1], rzs.at[g, d], rzr.at[g, d],
                      at(y, lax.rem(z + d, COLS)))

    def send_row(g):
        for d in range(1, COLS):
            z_send[g, d - 1] = row_acc[g, lax.rem(z + d, COLS)].astype(jnp.bfloat16)
            reduce_copy(g, d).start()

    def out_copies(g):
        cols = pl.ds(g * HEAD, HEAD)
        return (
            remote(fin.at[g, pl.ds(0, BLOCK)], dk_out.at[0, :, cols], dks.at[g, 0], dkr.at[g, 0], behind),
            remote(fin.at[g, pl.ds(BLOCK, BLOCK)], dv_out.at[0, :, cols], dks.at[g, 1], dkr.at[g, 1], behind),
        )

    def finish(g):
        total = row_acc[g, z]
        for d in range(1, COLS):
            reduce_copy(g, d).wait_recv()
            total += z_in[g, d - 1].astype(jnp.float32)
        fin[g] = total.astype(jnp.bfloat16)
        for c in out_copies(g):
            c.start()

    def drain_in(g):
        for d in range(1, COLS):
            row_copy(g, d).wait_send()
        for yy in range(ROWS):
            @pl.when(y == yy)
            def _(yy=yy):
                for hi in range(yy + 1, ROWS):
                    far_copy(g, yy, hi).wait_send()
                    if yy == 0 and hi != 2:
                        first_copy(g, hi).wait_send()
                if yy == 1:
                    hand_copy(g).wait_send()

    def drain_slots(g):
        for yy in range(1, ROWS):
            @pl.when(y == yy)
            def _(yy=yy):
                if yy == 1 and not direct(g, yy):
                    lead_end_copy(g).wait_send()
                if yy == 2 and not direct(g, yy):
                    lead_copy(g).wait_send()
                for lo in range(yy):
                    y_copy(g, lo, yy).wait_send()

    def drain_row(g):
        for d in range(1, COLS):
            reduce_copy(g, d).wait_send()

    def drain_out(g):
        for c in out_copies(g):
            c.wait()

    def drain_lists():
        for lo in range(ROWS - 1):
            @pl.when(lo < y)
            def _(lo=lo):
                remote(id_tile, id_in.at[y], id_ss.at[lo], id_rs.at[y], at(lo, z)).wait_send()

    gather_row(0)
    read_lists()
    send_listed(0)
    hand_first(0)
    gather_row(1)
    send_listed(1)
    q_copy.wait()
    g_copy.wait()
    compute(0)
    hand_first(1)
    gather_row(2)
    send_listed(2)
    compute(1)
    hand_first(2)
    fold_first(0)
    gather_row(3)
    send_listed(3)
    pass_on(0)
    add_rows(0)
    send_row(0)
    compute(2)
    hand_first(3)
    fold_first(1)
    pass_on(1)
    compute(3)
    fold_first(2)
    add_rows(1)
    send_row(1)
    finish(0)
    pass_on(2)
    add_rows(2)
    send_row(2)
    finish(1)
    fold_first(3)
    pass_on(3)
    finish(2)
    drain_lists()
    for g in range(GROUPS):
        drain_in(g)
    for g in range(GROUPS - 1):
        drain_slots(g)
    add_rows(3)
    send_row(3)
    drain_slots(3)
    for g in range(GROUPS - 1):
        drain_dq(g)
        drain_row(g)
    for g in range(GROUPS - 2):
        drain_out(g)
    finish(3)

    drain_dq(3)
    drain_row(3)
    drain_out(2)
    drain_out(3)


def per_device(queries, key_heads, value_per_head, out_grads, segment_ids, block_lists, list_counts):
    bf, f32 = jnp.bfloat16, jnp.float32
    anywhere = pl.BlockSpec(memory_space=pl.ANY)
    vmem = pl.BlockSpec(memory_space=pltpu.VMEM)
    smem = pl.BlockSpec(memory_space=pltpu.SMEM)
    two = 2 * BLOCK
    dma = pltpu.SemaphoreType.DMA
    keys_n = LIST * BLOCK
    scratch = (
        [pltpu.VMEM((COLS, two, HEAD), bf)] * GROUPS
        + [pltpu.VMEM((ROWS - 1, 3, two, HEAD), bf)] * GROUPS
        + [
            pltpu.VMEM((8, BLOCK), jnp.int32),
            pltpu.VMEM((ROWS, 8, BLOCK), jnp.int32),
            pltpu.SMEM((ROWS, 8, BLOCK), jnp.int32),
            pltpu.VMEM((BLOCK, QUERY_HEADS * HEAD), bf),
            pltpu.VMEM((BLOCK, QUERY_HEADS * HEAD), bf),
            pltpu.VMEM((GROUPS, ROWS - 1, 2, two, HEAD), bf),
            pltpu.VMEM((BLOCK, BLOCK), f32),
            pltpu.VMEM((keys_n, HEAD), bf),
            pltpu.VMEM((keys_n, HEAD), bf),
            pltpu.VMEM((HEAD, keys_n), bf),
            pltpu.VMEM((keys_n, HEAD), f32),
            pltpu.VMEM((keys_n, HEAD), f32),
            pltpu.VMEM((BLOCK, QUERY_HEADS * HEAD), bf),
            pltpu.VMEM((GROUPS, 3, two, HEAD), bf),
            pltpu.VMEM((GROUPS, ROWS - 1, 3, two, HEAD), bf),
            pltpu.VMEM((GROUPS, COLS, two, HEAD), f32),
            pltpu.VMEM((GROUPS, COLS - 1, two, HEAD), bf),
            pltpu.VMEM((GROUPS, COLS - 1, two, HEAD), bf),
            pltpu.VMEM((GROUPS, two, HEAD), bf),
            pltpu.VMEM((GROUPS, BLOCK // 4, GROUP_WIDTH), bf),
            pltpu.VMEM((GROUPS, two, HEAD), bf),
            pltpu.VMEM((GROUPS, two, HEAD), bf),
            dma((ROWS,)), dma((ROWS,)), dma((ROWS,)), dma((2,)), dma((GROUPS, 2)),
            dma((GROUPS, COLS)), dma((GROUPS, COLS)),
            dma((GROUPS, ROWS, ROWS)), dma((GROUPS, ROWS)),
            dma((GROUPS, ROWS)), dma((GROUPS,)),
            dma((GROUPS, ROWS)), dma((GROUPS, ROWS)),
            dma((GROUPS, COLS)), dma((GROUPS, COLS)),
            dma((GROUPS, 4)), dma((GROUPS, 4)),
            dma((GROUPS, 2)), dma((GROUPS, 2)),
            dma((GROUPS,)), dma((GROUPS,)), dma((GROUPS,)),
            dma((GROUPS,)), dma((GROUPS,)), dma((GROUPS,)), dma((GROUPS,)),
        ]
    )
    return pl.pallas_call(
        body,
        name="attention_grads",
        out_shape=(
            jax.ShapeDtypeStruct(queries.shape, bf),
            jax.ShapeDtypeStruct(key_heads.shape, bf),
            jax.ShapeDtypeStruct(value_per_head.shape, bf),
        ),
        in_specs=[smem, smem, vmem, anywhere, anywhere, anywhere, anywhere],
        out_specs=(anywhere, anywhere, anywhere),
        scratch_shapes=scratch,
        compiler_params=pltpu.CompilerParams(
            collective_id=0, has_side_effects=True, vmem_limit_bytes=48 << 20
        ),
    )(
        block_lists.reshape(LIST), list_counts.reshape(1), segment_ids,
        *(pltpu.with_memory_space_constraint(a, pltpu.HBM)
          for a in (key_heads, value_per_head, queries, out_grads)),
    )


def solution(mesh):
    rows = P("section", "blk", None)
    flat = P("section", "blk")
    return jax.shard_map(
        per_device,
        mesh=mesh,
        in_specs=(rows, rows, rows, rows, flat, rows, flat),
        out_specs=(rows, rows, rows),
        check_vma=False,
    )
```

```python
import functools
import math

import jax
import jax.numpy as jnp
from jax import lax
from jax.experimental import pallas as pl
from jax.experimental.pallas import tpu as pltpu
from jax.sharding import PartitionSpec as P

QUERY_HEADS = 32
GROUPS = 4
HEAD = 128
BLOCK = 128
LIST = 4
PER_GROUP = QUERY_HEADS // GROUPS
GROUP_WIDTH = PER_GROUP * HEAD
ROWS = 4
COLS = 4
NEG_FILL = -1e30
SCALE = 1.0 / math.sqrt(HEAD)
EXP2_SCALE = SCALE * math.log2(math.e)
MESH = pl.DeviceIdType.MESH


def body(
    lists, counts, segs, keys, values, queries, grads,
    dq_out, dk_out, dv_out,
    row0, row1, row2, row3, far0, far1, far2, far3,
    id_tile, id_in, id_smem,
    q_buf, g_buf, stage, mask0, kc, vc, kt, dk_acc, dv_acc, dq_buf,
    y_send, y_in, row_acc, z_send, z_in, fin, transit, lead_in, lead_out,
    id_ss, id_rs, id_ls, qg_s, kv_s,
    zs, zr, ys, yr, bs, br, rys, ryr, rzs, rzr, dqs, dqr, dks, dkr, trs, trr, tfs,
    lis, lir, los, lor,
):
    rowkv = (row0, row1, row2, row3)
    far = (far0, far1, far2, far3)
    sec = lax.axis_index("section")
    blk = lax.axis_index("blk")
    sections = lax.axis_size("section")
    y = blk // COLS
    z = lax.rem(blk, COLS)

    def at(yy, zz):
        return (sec, yy * COLS + zz)

    def remote(src, dst, ssem, rsem, dev):
        return pltpu.make_async_remote_copy(
            src_ref=src, dst_ref=dst, send_sem=ssem, recv_sem=rsem,
            device_id=dev, device_id_type=MESH,
        )

    here = (sec, blk)
    behind = (lax.rem(sec + sections - 1, sections), blk)
    ahead = (lax.rem(sec + 1, sections), blk)

    half = sec // 8
    x = lax.rem(sec, 8) // 2
    core = lax.rem(sec, 2)
    wraps = lax.rem(sec, 8) == 0
    relays = (core == 1) & (x > 0)
    lands = (core == 1) & (x == 3)
    relay_from = (half * 8, blk)
    relay_to = (lax.rem(half + 1, 2) * 8 + 7, blk)

    def relay_at(q):
        return (half * 8 + 2 * q + 1, blk)

    own_kv = []
    for g in range(GROUPS):
        cols = pl.ds(g * HEAD, HEAD)
        own_kv.append(pltpu.make_async_copy(keys.at[0, :, cols], rowkv[g].at[z, pl.ds(0, BLOCK)], kv_s.at[g, 0]))
        own_kv.append(pltpu.make_async_copy(values.at[0, :, cols], rowkv[g].at[z, pl.ds(BLOCK, BLOCK)], kv_s.at[g, 1]))
    for c in own_kv:
        c.start()

    q_copy = pltpu.make_async_copy(queries.at[0], q_buf, qg_s.at[0])
    g_copy = pltpu.make_async_copy(grads.at[0], g_buf, qg_s.at[1])
    q_copy.start()
    g_copy.start()

    barrier = pltpu.get_barrier_semaphore()
    peers = [behind, ahead]
    for d in (1, 2, 3):
        peers.append(at(y, lax.rem(z + d, COLS)))
    for d in (1, 2, 3):
        peers.append(at(lax.rem(y + d, ROWS), z))
    for p in peers:
        pl.semaphore_signal(barrier, inc=1, device_id=p, device_id_type=MESH)

    @pl.when(wraps)
    def _():
        for q in range(1, ROWS):
            pl.semaphore_signal(barrier, inc=1, device_id=relay_at(q), device_id_type=MESH)

    @pl.when(relays)
    def _():
        pl.semaphore_signal(barrier, inc=1, device_id=relay_from, device_id_type=MESH)
        pl.semaphore_signal(barrier, inc=1, device_id=relay_to, device_id_type=MESH)

    @pl.when(lands)
    def _():
        for q in range(1, ROWS):
            other = (lax.rem(half + 1, 2) * 8 + 2 * q + 1, blk)
            pl.semaphore_signal(barrier, inc=1, device_id=other, device_id_type=MESH)

    lanes = lax.broadcasted_iota(jnp.int32, (8, BLOCK), 0)
    tile = jnp.zeros((8, BLOCK), jnp.int32)
    for s in range(LIST):
        tile = jnp.where(lanes == s, lists[s], tile)
    id_tile[...] = tile
    for c in own_kv:
        c.wait()
    greeted = len(peers) + jnp.where(wraps | lands, 3, 0) + jnp.where(relays, 2, 0)
    pl.semaphore_wait(barrier, greeted)

    for lo in range(ROWS - 1):
        @pl.when(lo < y)
        def _(lo=lo):
            remote(id_tile, id_in.at[y], id_ss.at[lo], id_rs.at[y], at(lo, z)).start()

    def row_copy(g, d):
        return remote(rowkv[g].at[z], rowkv[g].at[z], zs.at[g, d], zr.at[g, d],
                      at(y, lax.rem(z + d, COLS)))

    def start_row(g):
        for d in range(1, COLS):
            row_copy(g, d).start()

    start_row(0)

    seg_row = jnp.broadcast_to(segs[...].astype(jnp.float32), (BLOCK, BLOCK))
    seg_col = seg_row.T
    key_pos = lax.broadcasted_iota(jnp.int32, (BLOCK, BLOCK), 0)
    query_pos = lax.broadcasted_iota(jnp.int32, (BLOCK, BLOCK), 1)
    mask0[...] = jnp.where((key_pos <= query_pos) & (seg_row == seg_col), 1.0, 0.0)

    def read_lists():
        copies = {hi: pltpu.make_async_copy(id_in.at[hi], id_smem.at[hi], id_ls.at[hi]) for hi in range(1, ROWS)}
        for hi in range(1, ROWS):
            @pl.when(hi > y)
            def _(hi=hi):
                remote(id_tile, id_in.at[hi], id_ss.at[0], id_rs.at[hi], here).wait_recv()
                copies[hi].start()
        for hi in range(1, ROWS):
            @pl.when(hi > y)
            def _(hi=hi):
                copies[hi].wait()

    own_id = [lists[s] for s in range(LIST)]
    count = counts[0]

    def gather_row(g):
        for d in range(1, COLS):
            row_copy(g, d).wait_recv()
        if g + 1 < GROUPS:
            start_row(g + 1)

    def far_copy(g, lo, hi):
        return remote(stage.at[g, hi - 1], far[g].at[lo, pl.ds(1, 2)], ys.at[g, lo, hi - 1],
                      yr.at[g, lo], at(hi, z))

    def first_copy(g, hi):
        return remote(rowkv[g].at[0], far[g].at[0, 0], bs.at[g, hi - 1], br.at[g], at(hi, z))

    def hand_copy(g):
        return remote(far[g].at[0, 0], far[g].at[0, 0], bs.at[g, 1], br.at[g], at(2, z))

    def hand_first(g):
        @pl.when(y == 1)
        def _():
            first_copy(g, 1).wait_recv()
            hand_copy(g).start()

    def send_listed(g):
        @pl.when(y == 0)
        def _():
            for hi in (1, 3):
                first_copy(g, hi).start()
        for lo in range(ROWS - 1):
            @pl.when(y == lo)
            def _(lo=lo):
                for hi in sorted(range(lo + 1, ROWS), reverse=True):
                    for s in (2, 3):
                        idx = lax.rem(id_smem[hi, s, 0], COLS)
                        stage[g, hi - 1, s - 2] = rowkv[g][idx]
                    far_copy(g, lo, hi).start()

    def pick(g, s):
        block = own_id[s]
        r, c = block // COLS, lax.rem(block, COLS)
        near = rowkv[g][c]
        away = far[g][jnp.minimum(r, ROWS - 2), s - 1]
        return jnp.where(r == y, near, away)

    def direct(g, hi):
        return hi == 3

    def y_copy(g, lo, hi):
        src, dst = (y_send.at[g], y_in.at[g, hi - 1]) if lo == 0 and direct(g, hi) else (
            y_send.at[g, pl.ds(1, 2)], y_in.at[g, hi - 1, pl.ds(1, 2)])
        return remote(src, dst, rys.at[g, lo], ryr.at[g, hi - 1], at(lo, z))

    def lead_copy(g):
        return remote(y_send.at[g, 0], lead_in.at[g], lis.at[g], lir.at[g], at(1, z))

    def lead_end_copy(g):
        return remote(lead_out.at[g], y_in.at[g, 0, 0], los.at[g], lor.at[g], at(0, z))

    def fold_first(g):
        @pl.when(y == 1)
        def _():
            lead_copy(g).wait_recv()
            total = y_send[g, 0].astype(jnp.float32) + lead_in[g].astype(jnp.float32)
            lead_out[g] = total.astype(jnp.bfloat16)
            lead_end_copy(g).start()

    def dq_copy(g, q, dev):
        part = (pl.ds(q * 32, 32), pl.ds(g * GROUP_WIDTH, GROUP_WIDTH))
        return remote(dq_buf.at[part], dq_out.at[(0,) + part], dqs.at[g, q], dqr.at[g, q], dev)

    def spread_copy(g, q):
        part = (pl.ds(q * 32, 32), pl.ds(g * GROUP_WIDTH, GROUP_WIDTH))
        return remote(dq_buf.at[part], transit.at[g], dqs.at[g, q], trr.at[g], relay_at(q))

    def pass_copy(g, q):
        part = (0, pl.ds(q * 32, 32), pl.ds(g * GROUP_WIDTH, GROUP_WIDTH))
        return remote(transit.at[g], dq_out.at[part], tfs.at[g], dqr.at[g, q], relay_to)

    def whole_copy(g):
        cols = pl.ds(g * GROUP_WIDTH, GROUP_WIDTH)
        return remote(dq_buf.at[:, cols], dq_out.at[0, :, cols], dqs.at[g, 0], dqr.at[g, 0], behind)

    def send_dq(g):
        @pl.when(wraps)
        def _():
            for q in range(1, ROWS):
                spread_copy(g, q).start()
            dq_copy(g, 0, behind).start()

        @pl.when(jnp.logical_not(wraps))
        def _():
            whole_copy(g).start()

    def drain_dq(g):
        @pl.when(wraps)
        def _():
            for q in range(ROWS):
                dq_copy(g, q, behind).wait_send()

        @pl.when(jnp.logical_not(wraps))
        def _():
            whole_copy(g).wait_send()

        @pl.when(lands)
        def _():
            for q in range(ROWS):
                dq_copy(g, q, behind).wait_recv()

        @pl.when(jnp.logical_not(lands))
        def _():
            whole_copy(g).wait_recv()
        for q in range(1, ROWS):
            @pl.when(relays & (x == q))
            def _(q=q):
                pass_copy(g, q).wait_send()

    def pass_on(g):
        for q in range(1, ROWS):
            @pl.when(relays & (x == q))
            def _(q=q):
                spread_copy(g, q).wait_recv()
                pass_copy(g, q).start()

    def compute(g):
        for lo in range(ROWS - 1):
            @pl.when(lo < y)
            def _(lo=lo):
                far_copy(g, lo, lo + 1).wait_recv()
        @pl.when(y > 1)
        def _():
            first_copy(g, 1).wait_recv()
        for s in range(LIST):
            if s == 0:
                both = rowkv[g][z]
            else:
                both = pick(g, s)
            kc[s * BLOCK:(s + 1) * BLOCK] = both[:BLOCK]
            vc[s * BLOCK:(s + 1) * BLOCK] = both[BLOCK:]
        kt[...] = kc[...].T
        dk_acc[...] = jnp.zeros_like(dk_acc)
        dv_acc[...] = jnp.zeros_like(dv_acc)
        diag = mask0[...] > 0.0
        diag2 = jnp.concatenate([diag, diag], axis=1)
        open_slot = [None] + [
            jnp.where((s < count) & (own_id[s] < blk), 0.0, NEG_FILL) for s in range(1, LIST)
        ]

        @pl.loop(0, PER_GROUP // 2, unroll=True)
        def _(pair):
            lo = pl.multiple_of(g * GROUP_WIDTH + pair * 2 * HEAD, HEAD)
            first, second = pl.ds(lo, HEAD), pl.ds(pl.multiple_of(lo + HEAD, HEAD), HEAD)
            qp = jnp.concatenate([q_buf[:, first], q_buf[:, second]], axis=0)
            gp = jnp.concatenate([g_buf[:, first], g_buf[:, second]], axis=0)
            nt = (((1,), (1,)), ((), ()))
            s_all = lax.dot_general(kc[...], qp, nt, preferred_element_type=jnp.float32) * EXP2_SCALE
            dp = lax.dot_general(vc[...], gp, nt, preferred_element_type=jnp.float32)
            parts = [jnp.where(diag2, s_all[:BLOCK], NEG_FILL)]
            for s in range(1, LIST):
                parts.append(s_all[s * BLOCK:(s + 1) * BLOCK] + open_slot[s])
            s_all = jnp.concatenate(parts, axis=0)
            top = jnp.max(s_all, axis=0, keepdims=True)
            w = jnp.exp2(s_all - top)
            p = w * (1.0 / jnp.sum(w, axis=0, keepdims=True))
            delta = jnp.sum(p * dp, axis=0, keepdims=True)
            ds = (p * (dp - delta)).astype(jnp.bfloat16)
            ph = p.astype(jnp.bfloat16)
            dk_acc[...] += jnp.dot(ds, qp, preferred_element_type=jnp.float32)
            dv_acc[...] += jnp.dot(ph, gp, preferred_element_type=jnp.float32)
            dqt = jnp.dot(kt[...], ds, preferred_element_type=jnp.float32) * SCALE
            dq = dqt.T.astype(jnp.bfloat16)
            dq_buf[:, first] = dq[:BLOCK]
            dq_buf[:, second] = dq[BLOCK:]

        for s in range(1, LIST):
            rows = slice(s * BLOCK, (s + 1) * BLOCK)
            y_send[g, s - 1, :BLOCK] = (dk_acc[rows] * SCALE).astype(jnp.bfloat16)
            y_send[g, s - 1, BLOCK:] = dv_acc[rows].astype(jnp.bfloat16)
        for hi in range(1, ROWS):
            @pl.when(y == hi)
            def _(hi=hi):
                if hi == 2 and not direct(g, hi):
                    lead_copy(g).start()
                for lo in range(hi):
                    y_copy(g, lo, hi).start()
        send_dq(g)
        for t in range(COLS):
            this = y * COLS + t
            for half, (acc, factor) in enumerate(((dk_acc, SCALE), (dv_acc, 1.0))):
                total = jnp.zeros((BLOCK, HEAD), jnp.float32)
                for s in range(LIST):
                    total += jnp.where(own_id[s] == this, acc[s * BLOCK:(s + 1) * BLOCK], 0.0)
                row_acc[g, t, half * BLOCK:(half + 1) * BLOCK] = total * factor

    def add_rows(g):
        for hi in range(1, ROWS):
            @pl.when(hi > y)
            def _(hi=hi):
                @pl.when(y == 0)
                def _():
                    y_copy(g, 0, hi).wait_recv()
                    if hi == 1 and not direct(g, hi):
                        lead_end_copy(g).wait_recv()
                @pl.when(y > 0)
                def _():
                    y_copy(g, 1, hi).wait_recv()
                for t in range(COLS):
                    total = row_acc[g, t]
                    for s in (2, 3):
                        hit = id_smem[hi, s, 0] == y * COLS + t
                        total += jnp.where(hit, y_in[g, hi - 1, s - 1].astype(jnp.float32), 0.0)
                    row_acc[g, t] = total
                if hi != 2 or direct(g, hi):
                    @pl.when(y == 0)
                    def _():
                        row_acc[g, 0] += y_in[g, hi - 1, 0].astype(jnp.float32)

    def reduce_copy(g, d):
        return remote(z_send.at[g, d - 1], z_in.at[g, d - 1], rzs.at[g, d], rzr.at[g, d],
                      at(y, lax.rem(z + d, COLS)))

    def send_row(g):
        for d in range(1, COLS):
            z_send[g, d - 1] = row_acc[g, lax.rem(z + d, COLS)].astype(jnp.bfloat16)
            reduce_copy(g, d).start()

    def out_copies(g):
        cols = pl.ds(g * HEAD, HEAD)
        return (
            remote(fin.at[g, pl.ds(0, BLOCK)], dk_out.at[0, :, cols], dks.at[g, 0], dkr.at[g, 0], behind),
            remote(fin.at[g, pl.ds(BLOCK, BLOCK)], dv_out.at[0, :, cols], dks.at[g, 1], dkr.at[g, 1], behind),
        )

    def finish(g):
        total = row_acc[g, z]
        for d in range(1, COLS):
            reduce_copy(g, d).wait_recv()
            total += z_in[g, d - 1].astype(jnp.float32)
        fin[g] = total.astype(jnp.bfloat16)
        for c in out_copies(g):
            c.start()

    def drain_in(g):
        for d in range(1, COLS):
            row_copy(g, d).wait_send()
        for yy in range(ROWS):
            @pl.when(y == yy)
            def _(yy=yy):
                for hi in range(yy + 1, ROWS):
                    far_copy(g, yy, hi).wait_send()
                    if yy == 0 and hi != 2:
                        first_copy(g, hi).wait_send()
                if yy == 1:
                    hand_copy(g).wait_send()

    def drain_slots(g):
        for yy in range(1, ROWS):
            @pl.when(y == yy)
            def _(yy=yy):
                if yy == 1 and not direct(g, yy):
                    lead_end_copy(g).wait_send()
                if yy == 2 and not direct(g, yy):
                    lead_copy(g).wait_send()
                for lo in range(yy):
                    y_copy(g, lo, yy).wait_send()

    def drain_row(g):
        for d in range(1, COLS):
            reduce_copy(g, d).wait_send()

    def drain_out(g):
        for c in out_copies(g):
            c.wait()

    def drain_lists():
        for lo in range(ROWS - 1):
            @pl.when(lo < y)
            def _(lo=lo):
                remote(id_tile, id_in.at[y], id_ss.at[lo], id_rs.at[y], at(lo, z)).wait_send()

    gather_row(0)
    read_lists()
    send_listed(0)
    hand_first(0)
    gather_row(1)
    send_listed(1)
    q_copy.wait()
    g_copy.wait()
    compute(0)
    hand_first(1)
    gather_row(2)
    send_listed(2)
    compute(1)
    hand_first(2)
    fold_first(0)
    gather_row(3)
    send_listed(3)
    pass_on(0)
    add_rows(0)
    send_row(0)
    compute(2)
    hand_first(3)
    fold_first(1)
    pass_on(1)
    compute(3)
    fold_first(2)
    add_rows(1)
    send_row(1)
    finish(0)
    pass_on(2)
    add_rows(2)
    send_row(2)
    fold_first(3)
    finish(1)
    pass_on(3)
    finish(2)
    drain_lists()
    for g in range(GROUPS):
        drain_in(g)
    for g in range(GROUPS - 1):
        drain_slots(g)
    add_rows(3)
    send_row(3)
    drain_slots(3)
    for g in range(GROUPS - 1):
        drain_dq(g)
        drain_row(g)
    for g in range(GROUPS - 2):
        drain_out(g)
    finish(3)

    drain_dq(3)
    drain_row(3)
    drain_out(2)
    drain_out(3)


def per_device(queries, key_heads, value_per_head, out_grads, segment_ids, block_lists, list_counts):
    bf, f32 = jnp.bfloat16, jnp.float32
    anywhere = pl.BlockSpec(memory_space=pl.ANY)
    vmem = pl.BlockSpec(memory_space=pltpu.VMEM)
    smem = pl.BlockSpec(memory_space=pltpu.SMEM)
    two = 2 * BLOCK
    dma = pltpu.SemaphoreType.DMA
    keys_n = LIST * BLOCK
    scratch = (
        [pltpu.VMEM((COLS, two, HEAD), bf)] * GROUPS
        + [pltpu.VMEM((ROWS - 1, 3, two, HEAD), bf)] * GROUPS
        + [
            pltpu.VMEM((8, BLOCK), jnp.int32),
            pltpu.VMEM((ROWS, 8, BLOCK), jnp.int32),
            pltpu.SMEM((ROWS, 8, BLOCK), jnp.int32),
            pltpu.VMEM((BLOCK, QUERY_HEADS * HEAD), bf),
            pltpu.VMEM((BLOCK, QUERY_HEADS * HEAD), bf),
            pltpu.VMEM((GROUPS, ROWS - 1, 2, two, HEAD), bf),
            pltpu.VMEM((BLOCK, BLOCK), f32),
            pltpu.VMEM((keys_n, HEAD), bf),
            pltpu.VMEM((keys_n, HEAD), bf),
            pltpu.VMEM((HEAD, keys_n), bf),
            pltpu.VMEM((keys_n, HEAD), f32),
            pltpu.VMEM((keys_n, HEAD), f32),
            pltpu.VMEM((BLOCK, QUERY_HEADS * HEAD), bf),
            pltpu.VMEM((GROUPS, 3, two, HEAD), bf),
            pltpu.VMEM((GROUPS, ROWS - 1, 3, two, HEAD), bf),
            pltpu.VMEM((GROUPS, COLS, two, HEAD), f32),
            pltpu.VMEM((GROUPS, COLS - 1, two, HEAD), bf),
            pltpu.VMEM((GROUPS, COLS - 1, two, HEAD), bf),
            pltpu.VMEM((GROUPS, two, HEAD), bf),
            pltpu.VMEM((GROUPS, BLOCK // 4, GROUP_WIDTH), bf),
            pltpu.VMEM((GROUPS, two, HEAD), bf),
            pltpu.VMEM((GROUPS, two, HEAD), bf),
            dma((ROWS,)), dma((ROWS,)), dma((ROWS,)), dma((2,)), dma((GROUPS, 2)),
            dma((GROUPS, COLS)), dma((GROUPS, COLS)),
            dma((GROUPS, ROWS, ROWS)), dma((GROUPS, ROWS)),
            dma((GROUPS, ROWS)), dma((GROUPS,)),
            dma((GROUPS, ROWS)), dma((GROUPS, ROWS)),
            dma((GROUPS, COLS)), dma((GROUPS, COLS)),
            dma((GROUPS, 4)), dma((GROUPS, 4)),
            dma((GROUPS, 2)), dma((GROUPS, 2)),
            dma((GROUPS,)), dma((GROUPS,)), dma((GROUPS,)),
            dma((GROUPS,)), dma((GROUPS,)), dma((GROUPS,)), dma((GROUPS,)),
        ]
    )
    return pl.pallas_call(
        body,
        name="attention_grads",
        out_shape=(
            jax.ShapeDtypeStruct(queries.shape, bf),
            jax.ShapeDtypeStruct(key_heads.shape, bf),
            jax.ShapeDtypeStruct(value_per_head.shape, bf),
        ),
        in_specs=[smem, smem, vmem, anywhere, anywhere, anywhere, anywhere],
        out_specs=(anywhere, anywhere, anywhere),
        scratch_shapes=scratch,
        compiler_params=pltpu.CompilerParams(
            collective_id=0, has_side_effects=True, vmem_limit_bytes=48 << 20
        ),
    )(
        block_lists.reshape(LIST), list_counts.reshape(1), segment_ids,
        *(pltpu.with_memory_space_constraint(a, pltpu.HBM)
          for a in (key_heads, value_per_head, queries, out_grads)),
    )


def solution(mesh):
    rows = P("section", "blk", None)
    flat = P("section", "blk")
    return jax.shard_map(
        per_device,
        mesh=mesh,
        in_specs=(rows, rows, rows, rows, flat, rows, flat),
        out_specs=(rows, rows, rows),
        check_vma=False,
    )
```
